32 devices in a mesh: groups: 1, mode: 32 (over z, y, x, core).
Axes of the slice: x: 2, y: 2, z: 4, core: 2. Of those that a mesh axis runs over, the one named last changes fastest.
Arguments:
- basis: bfloat16 [384, 16384], P('groups', 'mode')
- slab_region: int32 [128], P(('groups', 'mode')), may hold values from 0 to 8
- coef_index: int32 [9, 6], P('groups'), may hold values from 0 to 8
- coef_table: float32 [8], P('groups'), may hold values from 0.2 to 5
Outputs:
- gram: float32 [21, 384, 384], P(None, ('groups', 'mode'))
The draws below stay inside these ranges and needn't reach their ends.
All inputs are finite; a program needn't handle non-finite values.
Results may differ from the reference program's by a relative error of at most 0.0005.
The reference program's roundings to bfloat16 on the way (of `actions`) count: a program that leaves them out, or rounds other values in their place, can miss the bound.
Values may be sent and summed in bfloat16 or wider, within the bound.
A program may use at most 128 MiB of HBM per device.

```python
import math
import jax
import jax.numpy as jnp
from jax import lax

NB = 384
SLABW = 128
REGIONS = 9
TERMS = 6
NCOEF = 8
SLABS = 128
CELLS = 16384
N_MODE = 32


def draw_basis(key, part):
    key_mode = jax.random.fold_in(jax.random.fold_in(key, 17), 0)
    key_cell = jax.random.fold_in(jax.random.fold_in(key, 17), 1)
    key_main = jax.random.fold_in(jax.random.fold_in(key, 17), 2)
    key_pair = jax.random.fold_in(jax.random.fold_in(key, 17), 4)
    mode_scale = jnp.exp(math.log(10.0) * jax.random.uniform(key_mode, (NB,), jnp.float32) - math.log(10.0) * 0.5)
    ramp = jnp.arange(CELLS, dtype=jnp.float32) / CELLS
    cell_scale = jnp.exp(math.log(3.0) * ramp + math.log(3.0) * jax.random.uniform(key_cell, (CELLS,), jnp.float32))
    cell_block = jnp.arange(CELLS, dtype=jnp.int32) // (CELLS // N_MODE)
    mode_block = jnp.arange(NB, dtype=jnp.int32) // (NB // N_MODE)
    pairing = jax.random.permutation(key_pair, N_MODE)
    boost = jnp.where(pairing[cell_block][None, :] == mode_block[:, None], 4.0, 1.0)
    values = jnp.clip(jax.random.normal(key_main, (NB, CELLS), jnp.float32), -6.0, 6.0)
    return (boost * mode_scale[:, None] * cell_scale[None, :] * values).astype(jnp.bfloat16)


def touch_ends(values, rng, least, largest):
    longest = values.shape.index(max(values.shape))
    spots = []
    for shift in (0, 1):
        where = [jax.random.randint(jax.random.fold_in(rng, axis), (), 0, length) for axis, length in enumerate(values.shape)]
        where[longest] = (where[longest] + shift) % values.shape[longest]
        spots.append(tuple(where))
    return values.at[spots[0]].set(least).at[spots[1]].set(largest)


def setup_inputs(seed: int = 0, part: int = 0) -> dict:
    arg_keys = jax.random.split(jax.random.key(seed), 5)
    own_keys = jax.random.split(jax.random.fold_in(arg_keys[4], part), 5)
    basis = draw_basis(jax.random.fold_in(jax.random.fold_in(arg_keys[4], part), 71), part)
    slab_region = touch_ends(jax.random.randint(own_keys[1], (SLABS,), 0, REGIONS), jax.random.fold_in(own_keys[1], 1), 0, REGIONS - 1).astype(jnp.int32)
    coef_index = touch_ends(jax.random.randint(own_keys[2], (REGIONS, TERMS), 0, NCOEF + 1), jax.random.fold_in(own_keys[2], 1), 0, NCOEF).astype(jnp.int32)
    coef_table = jnp.clip(jnp.exp(jax.random.uniform(own_keys[3], (NCOEF,), jnp.float32, math.log(0.2), math.log(5.0))), 0.2, 5.0)
    return {"basis": basis, "slab_region": slab_region, "coef_index": coef_index, "coef_table": coef_table}


def slab_weights(slab_region, coef_index, coef_table):
    table_hit = (coef_index[:, :, None] == jnp.arange(NCOEF, dtype=jnp.int32)[None, None, :]).astype(jnp.float32)
    kappa = lax.optimization_barrier(jnp.sum(table_hit * coef_table[None, None, :], axis=2))
    region_hit = (slab_region[:, None] == jnp.arange(REGIONS, dtype=jnp.int32)[None, :]).astype(jnp.float32)
    return lax.optimization_barrier(jnp.sum(region_hit[:, :, None] * kappa[None, :, :], axis=1))

def one_action(field, weight, term):
    rows = field.shape[0]
    if term == 0:
        stencil = 2.0 * field - jnp.roll(field, 1, axis=1) - jnp.roll(field, -1, axis=1)
    elif term == 1:
        zero_col = jnp.zeros((rows, SLABS, 1), jnp.float32)
        left_w = jnp.concatenate([zero_col, field[:, :, :-1]], axis=2)
        right_w = jnp.concatenate([field[:, :, 1:], zero_col], axis=2)
        stencil = 2.0 * field - left_w - right_w
    elif term == 2:
        stencil = field - jnp.roll(field, 1, axis=1)
    elif term == 3:
        stencil = field - jnp.roll(field, -1, axis=1)
    elif term == 4:
        stencil = field - field[:, :, ::-1]
    else:
        stencil = field
    return (weight[None, :, None] * stencil).reshape(rows, SLABS * SLABW).astype(jnp.bfloat16)

def reference(basis, slab_region, coef_index, coef_table):
    slab_kappa = slab_weights(slab_region, coef_index, coef_table)
    field = basis.astype(jnp.float32).reshape(NB, SLABS, SLABW)
    actions = [one_action(field, slab_kappa[:, term], term) for term in range(TERMS)]
    sums = []
    for term in range(TERMS):
        values = actions[term].astype(jnp.float32)
        sums.append(jnp.sum(values * values))
    level = jnp.stack(sums) / (NB * CELLS) + 1e-06
    blocks = []
    for first in range(TERMS):
        for second in range(first, TERMS):
            raw = jnp.dot(actions[first], actions[second].T, preferred_element_type=jnp.float32)
            blocks.append(raw / (CELLS * jnp.sqrt(level[first] * level[second])))
    return jnp.stack(blocks, axis=0)
```

```python
import jax
import jax.numpy as jnp
from jax import lax
from jax.sharding import PartitionSpec as P


def plane_size(devices, share):
    size = 1
    while (
        4 * size * size <= 2 * devices
        and devices % (2 * size) == 0
        and 2 * size * share <= 24 << 20
    ):
        size *= 2
    return size


def slab_weights(slab_region, coef_index, coef_table):
    regions = coef_index.shape[0]
    entries = coef_table.shape[0]
    table_hit = (
        coef_index[:, :, None] == jnp.arange(entries, dtype=jnp.int32)[None, None, :]
    ).astype(jnp.float32)
    kappa = jnp.sum(table_hit * coef_table[None, None, :], axis=2)
    region_hit = (slab_region[:, None] == jnp.arange(regions, dtype=jnp.int32)[None, :]).astype(
        jnp.float32
    )
    return jnp.sum(region_hit[:, :, None] * kappa[None, :, :], axis=1)


def term_actions(field, low, high, slab_kappa):
    rows, slabs, width = field.shape
    terms = slab_kappa.shape[1]
    prev_s = jnp.concatenate([low, field[:, :-1]], axis=1).astype(jnp.float32)
    next_s = jnp.concatenate([field[:, 1:], high], axis=1).astype(jnp.float32)
    field = field.astype(jnp.float32)
    zero_col = jnp.zeros((rows, slabs, 1), jnp.float32)
    left_w = jnp.concatenate([zero_col, field[:, :, :-1]], axis=2)
    right_w = jnp.concatenate([field[:, :, 1:], zero_col], axis=2)
    mirror = field[:, :, ::-1]
    stencils = [
        2.0 * field - prev_s - next_s,
        2.0 * field - left_w - right_w,
        field - prev_s,
        field - next_s,
        field - mirror,
        field,
    ]
    return [
        (slab_kappa[None, :, term, None] * stencils[term])
        .reshape(rows, slabs * width)
        .astype(jnp.bfloat16)
        for term in range(terms)
    ]


def per_device(basis, slab_region, coef_index, coef_table):
    terms = coef_index.shape[1]
    rows, cells_dev = basis.shape
    slabs_dev = slab_region.shape[0]
    width = cells_dev // slabs_dev
    devices = lax.axis_size("mode")
    total_cells = cells_dev * devices
    inner = plane_size(devices, 2 * terms * rows * cells_dev)
    outer = devices // inner
    own = rows // devices
    slabs = slabs_dev * inner
    planes = [[a * inner + c for c in range(inner)] for a in range(outer)]
    columns = [[a * inner + c for a in range(outer)] for c in range(inner)]
    tags = jnp.broadcast_to(
        slab_region.astype(jnp.bfloat16)[None, :, None], (16, slabs_dev, width)
    ).reshape(16, cells_dev)
    packed = lax.all_gather(
        jnp.concatenate([basis, tags], axis=0), "mode", axis_index_groups=planes, axis=0
    )
    packed = jnp.transpose(packed, (1, 0, 2)).reshape(rows + 16, slabs, width)
    field = packed[:rows]
    region = packed[rows, :, 0].astype(jnp.int32)
    slab_kappa = slab_weights(region, coef_index, coef_table)
    up = [(i, (i + inner) % devices) for i in range(devices)]
    down = [(target, source) for source, target in up]
    low = lax.ppermute(field[:, -1:], "mode", up)
    high = lax.ppermute(field[:, :1], "mode", down)
    acts = term_actions(field, low, high, slab_kappa)
    column = lax.rem(lax.axis_index("mode"), inner)
    mine = []
    for act in acts:
        view = act.reshape(outer, inner, own, slabs * width)
        mine.append(
            lax.dynamic_index_in_dim(view, column, 1, keepdims=False).reshape(
                outer * own, slabs * width
            )
        )
    pair_list = [(first, second) for first in range(terms) for second in range(first, terms)]
    level_sums = lax.psum(
        jnp.stack([jnp.sum(jnp.square(v.astype(jnp.float32))) for v in mine]), "mode"
    )
    pieces = [
        lax.dot_general(
            mine[first], acts[second], (((1,), (1,)), ((), ())), preferred_element_type=jnp.float32
        )
        for first, second in pair_list
    ]
    raw = lax.psum_scatter(
        jnp.concatenate([p.reshape(outer, own, rows)[:, None] for p in pieces], axis=1),
        "mode",
        scatter_dimension=0,
        axis_index_groups=columns,
        tiled=True,
    )[0]
    level = level_sums / (rows * total_cells) + 1e-06
    factors = jnp.stack(
        [
            1.0 / (total_cells * jnp.sqrt(level[first] * level[second]))
            for first, second in pair_list
        ]
    )
    return raw.reshape(len(pair_list), own, rows) * factors[:, None, None]


def solution(mesh):
    return jax.shard_map(
        per_device,
        mesh=mesh,
        in_specs=(P("groups", "mode"), P(("groups", "mode")), P("groups", None), P("groups")),
        out_specs=P(None, ("groups", "mode"), None),
        check_vma=False,
    )
```

```python
import functools

import jax
import jax.numpy as jnp
from jax import lax
from jax.experimental import pallas as pl
from jax.experimental.pallas import tpu as pltpu
from jax.sharding import PartitionSpec as P


def plane_size(devices, share):
    size = 1
    while (
        4 * size * size <= 2 * devices
        and devices % (2 * size) == 0
        and 2 * size * share <= 24 << 20
    ):
        size *= 2
    return size


def slab_weights(slab_region, coef_index, coef_table):
    regions = coef_index.shape[0]
    entries = coef_table.shape[0]
    table_hit = (
        coef_index[:, :, None] == jnp.arange(entries, dtype=jnp.int32)[None, None, :]
    ).astype(jnp.float32)
    kappa = jnp.sum(table_hit * coef_table[None, None, :], axis=2)
    region_hit = (slab_region[:, None] == jnp.arange(regions, dtype=jnp.int32)[None, :]).astype(
        jnp.float32
    )
    return jnp.sum(region_hit[:, :, None] * kappa[None, :, :], axis=1)


def one_action(term, here, before, after, across, opposite, kappa):
    value = here.astype(jnp.float32)
    if term == 0:
        stencil = 2.0 * value - before.astype(jnp.float32) - after.astype(jnp.float32)
    elif term == 1:
        stencil = jnp.dot(here, across, preferred_element_type=jnp.float32)
    elif term == 2:
        stencil = value - before.astype(jnp.float32)
    elif term == 3:
        stencil = value - after.astype(jnp.float32)
    elif term == 4:
        stencil = jnp.dot(here, opposite, preferred_element_type=jnp.float32)
    else:
        stencil = value
    return (kappa * stencil).astype(jnp.bfloat16)


def gram_kernel(terms, inner, outer, own, slabs_dev, total_cells, *refs):
    basis, kap, out = refs[:3]
    field, weights, mine, lhs, act, acc = refs[3:9]
    stages = refs[9 : 9 + terms]
    arrived = refs[9 + terms : 9 + 2 * terms]
    lvl, lvl_col, lvl_mid, lvl_row = refs[9 + 2 * terms : 13 + 2 * terms]
    load_sem, gs, gr, ks, kr, hs, hr, zs, zr, cs, cr, rs, rr = refs[13 + 2 * terms :]
    rows, width = field.shape[1], field.shape[2]
    slabs = inner * slabs_dev
    local = outer * own
    me = lax.axis_index("mode")
    plane = me // inner
    column = me % inner

    def row_peer(d):
        return plane * inner + lax.rem(column + d, inner)

    def col_peer(d):
        return lax.rem(plane + d, outer) * inner + column

    def remote(src, dst, send, recv, peer):
        return pltpu.make_async_remote_copy(
            src_ref=src,
            dst_ref=dst,
            send_sem=send,
            recv_sem=recv,
            device_id={"mode": peer},
            device_id_type=pl.DeviceIdType.MESH,
        )

    loads = []
    for s in range(slabs_dev):
        loads.append(
            pltpu.make_async_copy(
                basis.at[:, pl.ds(s * width, width)],
                field.at[1 + column * slabs_dev + s],
                load_sem.at[s],
            )
        )
    loads.append(
        pltpu.make_async_copy(
            kap, weights.at[pl.ds(column * slabs_dev, slabs_dev)], load_sem.at[slabs_dev]
        )
    )
    for copy in loads:
        copy.start()

    barrier = pltpu.get_barrier_semaphore()
    for d in range(1, inner):
        pl.semaphore_signal(
            barrier, inc=1, device_id={"mode": row_peer(d)}, device_id_type=pl.DeviceIdType.MESH
        )
    for d in range(1, outer):
        pl.semaphore_signal(
            barrier, inc=1, device_id={"mode": col_peer(d)}, device_id_type=pl.DeviceIdType.MESH
        )
    pl.semaphore_wait(barrier, inner + outer - 2)
    for copy in loads:
        copy.wait()

    block = pl.ds(1 + column * slabs_dev, slabs_dev)
    spot = pl.ds(column * slabs_dev, slabs_dev)
    gathers = []
    for d in range(1, inner):
        gathers.append(
            remote(weights.at[spot], weights.at[spot], ks.at[d - 1], kr.at[d - 1], row_peer(d))
        )
        gathers.append(
            remote(field.at[block], field.at[block], gs.at[d - 1], gr.at[d - 1], row_peer(d))
        )
    for copy in gathers:
        copy.start()

    wi = lax.broadcasted_iota(jnp.int32, (width, width), 0)
    wj = lax.broadcasted_iota(jnp.int32, (width, width), 1)
    near = jnp.where((wi == wj + 1) | (wj == wi + 1), 1.0, 0.0)
    same = jnp.where(wi == wj, 1.0, 0.0)
    flip = jnp.where(wi + wj == width - 1, 1.0, 0.0)
    across = (2.0 * same - near).astype(jnp.bfloat16)
    opposite = (same - flip).astype(jnp.bfloat16)
    ri = lax.broadcasted_iota(jnp.int32, (local, rows), 0)
    rj = lax.broadcasted_iota(jnp.int32, (local, rows), 1)
    source = ri + column * own
    for a in range(1, outer):
        source = source + jnp.where(ri >= a * own, inner * own - own, 0)
    select = jnp.where(rj == source, 1.0, 0.0).astype(jnp.bfloat16)
    lvl[...] = jnp.zeros_like(lvl)

    for copy in gathers:
        copy.wait()
    halos = [
        remote(field.at[slabs], field.at[0], hs.at[0], hr.at[0], col_peer(1)),
        remote(field.at[1], field.at[slabs + 1], hs.at[1], hr.at[1], col_peer(outer - 1)),
    ]
    for copy in halos:
        copy.start()
    for copy in halos:
        copy.wait()

    @pl.loop(0, slabs + 2)
    def _(s):
        mine[s] = jnp.dot(select, field[s], preferred_element_type=jnp.float32).astype(
            jnp.bfloat16
        )

    @pl.loop(0, inner)
    def _(b):
        for s in range(slabs_dev):
            at = b * slabs_dev + s
            for term in range(terms):
                value = one_action(
                    term,
                    mine[at + 1],
                    mine[at],
                    mine[at + 2],
                    across,
                    opposite,
                    weights[at, term : term + 1, :],
                )
                lhs[b, term * local : (term + 1) * local, s * width : (s + 1) * width] = value
                wide = value.astype(jnp.float32)
                lvl[term : term + 1, :] += jnp.sum(wide * wide, axis=0, keepdims=True)

    cols = [
        remote(lvl, lvl_col.at[d - 1], cs.at[d - 1], cr.at[d - 1], col_peer(d))
        for d in range(1, outer)
    ]
    for copy in cols:
        copy.start()

    sends = []
    rowsends = []
    for turn, second in enumerate(reversed(range(terms))):
        deep = (second + 1) * local
        acc[0:deep, :] = jnp.zeros((deep, rows), jnp.float32)

        @pl.loop(0, inner)
        def _(b, second=second, deep=deep):
            for s in range(slabs_dev):
                at = b * slabs_dev + s
                act[:, s * width : (s + 1) * width] = one_action(
                    second,
                    field[at + 1],
                    field[at],
                    field[at + 2],
                    across,
                    opposite,
                    weights[at, second : second + 1, :],
                )
            acc[0:deep, :] += lax.dot_general(
                lhs[b, 0:deep, :],
                act[...],
                (((1,), (1,)), ((), ())),
                preferred_element_type=jnp.float32,
            )

        for a in range(outer):
            for first in range(second + 1):
                stages[second][a, first * own : (first + 1) * own, :] = acc[
                    first * local + a * own : first * local + (a + 1) * own, :
                ]
        for d in range(1, outer):
            n = second * (outer - 1) + d - 1
            copy = remote(
                stages[second].at[lax.rem(plane + d, outer)],
                arrived[second].at[d - 1],
                zs.at[n],
                zr.at[n],
                col_peer(d),
            )
            copy.start()
            sends.append((second, copy))
        if turn == 0:
            for copy in cols:
                copy.wait()
            mid = lvl[...]
            for d in range(1, outer):
                mid = mid + lvl_col[d - 1]
            lvl_mid[...] = mid
            rowsends = [
                remote(lvl_mid, lvl_row.at[d - 1], rs.at[d - 1], rr.at[d - 1], row_peer(d))
                for d in range(1, inner)
            ]
            for copy in rowsends:
                copy.start()

    for copy in rowsends:
        copy.wait()
    total = lvl_mid[...]
    for d in range(1, inner):
        total = total + lvl_row[d - 1]
    level = jnp.sum(total, axis=1, keepdims=True) / (rows * total_cells) + 1e-06
    for second in reversed(range(terms)):
        for q, copy in sends:
            if q == second:
                copy.wait()
        for first in range(second + 1):
            part = pl.ds(first * own, own)
            value = stages[second][plane, part, :]
            for d in range(1, outer):
                value = value + arrived[second][d - 1, part, :]
            factor = 1.0 / (
                total_cells * jnp.sqrt(level[first : first + 1] * level[second : second + 1])
            )
            pair = first * terms - first * (first - 1) // 2 + second - first
            out[pair] = value * factor


def per_device(basis, slab_region, coef_index, coef_table):
    terms = coef_index.shape[1]
    rows, cells_dev = basis.shape
    slabs_dev = slab_region.shape[0]
    width = cells_dev // slabs_dev
    devices = lax.axis_size("mode")
    inner = plane_size(devices, 2 * terms * rows * cells_dev)
    outer = devices // inner
    own = rows // devices
    slabs = slabs_dev * inner
    local = outer * own
    slab_kappa = slab_weights(slab_region, coef_index, coef_table)
    kap = jnp.broadcast_to(
        jnp.pad(slab_kappa, ((0, 0), (0, -terms % 8)))[:, :, None],
        (slabs_dev, terms + -terms % 8, width),
    )
    tall = terms + -terms % 8
    f32, b16 = jnp.float32, jnp.bfloat16
    deep = [(q + 1) * own for q in range(terms)]
    dma = pltpu.SemaphoreType.DMA
    return pl.pallas_call(
        functools.partial(
            gram_kernel, terms, inner, outer, own, slabs_dev, cells_dev * devices
        ),
        out_shape=jax.ShapeDtypeStruct((terms * (terms + 1) // 2, own, rows), f32),
        in_specs=[pl.BlockSpec(memory_space=pl.ANY)] * 2,
        out_specs=pl.BlockSpec(memory_space=pltpu.VMEM),
        scratch_shapes=[
            pltpu.VMEM((slabs + 2, rows, width), b16),
            pltpu.VMEM((slabs, tall, width), f32),
            pltpu.VMEM((slabs + 2, local, width), b16),
            pltpu.VMEM((inner, terms * local, cells_dev), b16),
            pltpu.VMEM((rows, cells_dev), b16),
            pltpu.VMEM((terms * local, rows), f32),
        ]
        + [pltpu.VMEM((outer, n, rows), f32) for n in deep]
        + [pltpu.VMEM((outer - 1, n, rows), f32) for n in deep]
        + [
            pltpu.VMEM((tall, width), f32),
            pltpu.VMEM((outer - 1, tall, width), f32),
            pltpu.VMEM((tall, width), f32),
            pltpu.VMEM((inner - 1, tall, width), f32),
            dma((slabs_dev + 1,)),
            dma((inner - 1,)),
            dma((inner - 1,)),
            dma((inner - 1,)),
            dma((inner - 1,)),
            dma((2,)),
            dma((2,)),
            dma((terms * (outer - 1),)),
            dma((terms * (outer - 1),)),
            dma((outer - 1,)),
            dma((outer - 1,)),
            dma((inner - 1,)),
            dma((inner - 1,)),
        ],
        compiler_params=pltpu.CompilerParams(
            collective_id=0, has_side_effects=True, vmem_limit_bytes=48 << 20
        ),
    )(basis, kap)


def solution(mesh):
    return jax.shard_map(
        per_device,
        mesh=mesh,
        in_specs=(P("groups", "mode"), P(("groups", "mode")), P("groups", None), P("groups")),
        out_specs=P(None, ("groups", "mode"), None),
        check_vma=False,
    )
```

```python
import functools

import jax
import jax.numpy as jnp
from jax import lax
from jax.experimental import pallas as pl
from jax.experimental.pallas import tpu as pltpu
from jax.sharding import PartitionSpec as P


def plane_size(devices, share):
    size = 1
    while (
        4 * size * size <= 2 * devices
        and devices % (2 * size) == 0
        and 2 * size * share <= 24 << 20
    ):
        size *= 2
    return size


def slab_weights(slab_region, coef_index, coef_table):
    regions = coef_index.shape[0]
    entries = coef_table.shape[0]
    table_hit = (
        coef_index[:, :, None] == jnp.arange(entries, dtype=jnp.int32)[None, None, :]
    ).astype(jnp.float32)
    kappa = jnp.sum(table_hit * coef_table[None, None, :], axis=2)
    region_hit = (slab_region[:, None] == jnp.arange(regions, dtype=jnp.int32)[None, :]).astype(
        jnp.float32
    )
    return jnp.sum(region_hit[:, :, None] * kappa[None, :, :], axis=1)


def one_action(term, here, before, after, across, opposite, kappa):
    value = here.astype(jnp.float32)
    if term == 0:
        stencil = 2.0 * value - before.astype(jnp.float32) - after.astype(jnp.float32)
    elif term == 1:
        stencil = jnp.dot(here, across, preferred_element_type=jnp.float32)
    elif term == 2:
        stencil = value - before.astype(jnp.float32)
    elif term == 3:
        stencil = value - after.astype(jnp.float32)
    elif term == 4:
        stencil = jnp.dot(here, opposite, preferred_element_type=jnp.float32)
    else:
        stencil = value
    return (kappa * stencil).astype(jnp.bfloat16)


def gram_kernel(terms, inner, outer, own, slabs_dev, total_cells, *refs):
    basis, kap, out = refs[:3]
    field, weights, mine, lhs, act, acc = refs[3:9]
    stages = refs[9 : 9 + terms]
    arrived = refs[9 + terms : 9 + 2 * terms]
    lvl, lvl_col, lvl_mid, lvl_row = refs[9 + 2 * terms : 13 + 2 * terms]
    load_sem, gs, gr, ks, kr, hs, hr, zs, zr, cs, cr, rs, rr = refs[13 + 2 * terms :]
    rows, width = field.shape[1], field.shape[2]
    slabs = inner * slabs_dev
    local = outer * own
    me = lax.axis_index("mode")
    plane = me // inner
    column = me % inner

    def row_peer(d):
        return plane * inner + lax.rem(column + d, inner)

    def col_peer(d):
        return lax.rem(plane + d, outer) * inner + column

    def remote(src, dst, send, recv, peer):
        return pltpu.make_async_remote_copy(
            src_ref=src,
            dst_ref=dst,
            send_sem=send,
            recv_sem=recv,
            device_id={"mode": peer},
            device_id_type=pl.DeviceIdType.MESH,
        )

    loads = []
    for s in range(slabs_dev):
        loads.append(
            pltpu.make_async_copy(
                basis.at[:, pl.ds(s * width, width)],
                field.at[1 + column * slabs_dev + s],
                load_sem.at[s],
            )
        )
    loads.append(
        pltpu.make_async_copy(
            kap, weights.at[pl.ds(column * slabs_dev, slabs_dev)], load_sem.at[slabs_dev]
        )
    )
    for copy in loads:
        copy.start()

    barrier = pltpu.get_barrier_semaphore()
    for d in range(1, inner):
        pl.semaphore_signal(
            barrier, inc=1, device_id={"mode": row_peer(d)}, device_id_type=pl.DeviceIdType.MESH
        )
    for d in range(1, outer):
        pl.semaphore_signal(
            barrier, inc=1, device_id={"mode": col_peer(d)}, device_id_type=pl.DeviceIdType.MESH
        )
    pl.semaphore_wait(barrier, inner + outer - 2)
    for copy in loads:
        copy.wait()

    chips = inner // 2
    chip = column // 2
    core = column % 2
    sibling = plane * inner + chip * 2 + 1 - core
    spot = pl.ds(column * slabs_dev, slabs_dev)
    small = [
        remote(weights.at[spot], weights.at[spot], ks.at[d - 1], kr.at[d - 1], row_peer(d))
        for d in range(1, inner)
    ]

    def push(origin, slot, peer):
        span = pl.ds(1 + origin * slabs_dev, slabs_dev)
        return remote(field.at[span], field.at[span], gs.at[slot], gr.at[slot], peer)

    far = [
        push(column, d, plane * inner + lax.rem(chip + d, chips) * 2 + core)
        for d in range(1, chips)
    ]
    gathers = [push(column, 0, sibling)]
    for copy in small + far + gathers:
        copy.start()

    wi = lax.broadcasted_iota(jnp.int32, (width, width), 0)
    wj = lax.broadcasted_iota(jnp.int32, (width, width), 1)
    near = jnp.where((wi == wj + 1) | (wj == wi + 1), 1.0, 0.0)
    same = jnp.where(wi == wj, 1.0, 0.0)
    flip = jnp.where(wi + wj == width - 1, 1.0, 0.0)
    across = (2.0 * same - near).astype(jnp.bfloat16)
    opposite = (same - flip).astype(jnp.bfloat16)
    ri = lax.broadcasted_iota(jnp.int32, (local, rows), 0)
    rj = lax.broadcasted_iota(jnp.int32, (local, rows), 1)
    source = ri + column * own
    for a in range(1, outer):
        source = source + jnp.where(ri >= a * own, inner * own - own, 0)
    select = jnp.where(rj == source, 1.0, 0.0).astype(jnp.bfloat16)
    lvl[...] = jnp.zeros_like(lvl)

    for d, copy in enumerate(far, 1):
        copy.wait_recv()
        origin = lax.rem(chip + chips - d, chips) * 2 + core
        relay = push(origin, chips - 1 + d, sibling)
        relay.start()
        gathers.append(relay)
    for copy in far:
        copy.wait_send()
    for copy in small + gathers:
        copy.wait()
    halos = [
        remote(field.at[slabs], field.at[0], hs.at[0], hr.at[0], col_peer(1)),
        remote(field.at[1], field.at[slabs + 1], hs.at[1], hr.at[1], col_peer(outer - 1)),
    ]
    for copy in halos:
        copy.start()
    for copy in halos:
        copy.wait()

    @pl.loop(0, slabs + 2)
    def _(s):
        mine[s] = jnp.dot(select, field[s], preferred_element_type=jnp.float32).astype(
            jnp.bfloat16
        )

    @pl.loop(0, inner)
    def _(b):
        for s in range(slabs_dev):
            at = b * slabs_dev + s
            for term in range(terms):
                value = one_action(
                    term,
                    mine[at + 1],
                    mine[at],
                    mine[at + 2],
                    across,
                    opposite,
                    weights[at, term : term + 1, :],
                )
                lhs[b, term * local : (term + 1) * local, s * width : (s + 1) * width] = value
                wide = value.astype(jnp.float32)
                lvl[term : term + 1, :] += jnp.sum(wide * wide, axis=0, keepdims=True)

    cols = [
        remote(lvl, lvl_col.at[d - 1], cs.at[d - 1], cr.at[d - 1], col_peer(d))
        for d in range(1, outer)
    ]
    for copy in cols:
        copy.start()

    sends = []
    rowsends = []
    for turn, second in enumerate(reversed(range(terms))):
        deep = (second + 1) * local
        acc[0:deep, :] = jnp.zeros((deep, rows), jnp.float32)

        @pl.loop(0, inner)
        def _(b, second=second, deep=deep):
            for s in range(slabs_dev):
                at = b * slabs_dev + s
                act[:, s * width : (s + 1) * width] = one_action(
                    second,
                    field[at + 1],
                    field[at],
                    field[at + 2],
                    across,
                    opposite,
                    weights[at, second : second + 1, :],
                )
            acc[0:deep, :] += lax.dot_general(
                lhs[b, 0:deep, :],
                act[...],
                (((1,), (1,)), ((), ())),
                preferred_element_type=jnp.float32,
            )

        for a in range(outer):
            for first in range(second + 1):
                stages[second][a, first * own : (first + 1) * own, :] = acc[
                    first * local + a * own : first * local + (a + 1) * own, :
                ]
        for d in range(1, outer):
            n = second * (outer - 1) + d - 1
            copy = remote(
                stages[second].at[lax.rem(plane + d, outer)],
                arrived[second].at[d - 1],
                zs.at[n],
                zr.at[n],
                col_peer(d),
            )
            copy.start()
            sends.append((second, copy))
        if turn == 0:
            for copy in cols:
                copy.wait()
            mid = lvl[...]
            for d in range(1, outer):
                mid = mid + lvl_col[d - 1]
            lvl_mid[...] = mid
            rowsends = [
                remote(lvl_mid, lvl_row.at[d - 1], rs.at[d - 1], rr.at[d - 1], row_peer(d))
                for d in range(1, inner)
            ]
            for copy in rowsends:
                copy.start()

    for copy in rowsends:
        copy.wait()
    total = lvl_mid[...]
    for d in range(1, inner):
        total = total + lvl_row[d - 1]
    level = jnp.sum(total, axis=1, keepdims=True) / (rows * total_cells) + 1e-06
    for second in reversed(range(terms)):
        for q, copy in sends:
            if q == second:
                copy.wait()
        for first in range(second + 1):
            part = pl.ds(first * own, own)
            value = stages[second][plane, part, :]
            for d in range(1, outer):
                value = value + arrived[second][d - 1, part, :]
            factor = 1.0 / (
                total_cells * jnp.sqrt(level[first : first + 1] * level[second : second + 1])
            )
            pair = first * terms - first * (first - 1) // 2 + second - first
            out[pair] = value * factor


def per_device(basis, slab_region, coef_index, coef_table):
    terms = coef_index.shape[1]
    rows, cells_dev = basis.shape
    slabs_dev = slab_region.shape[0]
    width = cells_dev // slabs_dev
    devices = lax.axis_size("mode")
    inner = plane_size(devices, 2 * terms * rows * cells_dev)
    outer = devices // inner
    own = rows // devices
    slabs = slabs_dev * inner
    local = outer * own
    slab_kappa = slab_weights(slab_region, coef_index, coef_table)
    kap = jnp.broadcast_to(
        jnp.pad(slab_kappa, ((0, 0), (0, -terms % 8)))[:, :, None],
        (slabs_dev, terms + -terms % 8, width),
    )
    tall = terms + -terms % 8
    f32, b16 = jnp.float32, jnp.bfloat16
    deep = [(q + 1) * own for q in range(terms)]
    dma = pltpu.SemaphoreType.DMA
    return pl.pallas_call(
        functools.partial(
            gram_kernel, terms, inner, outer, own, slabs_dev, cells_dev * devices
        ),
        out_shape=jax.ShapeDtypeStruct((terms * (terms + 1) // 2, own, rows), f32),
        in_specs=[pl.BlockSpec(memory_space=pl.ANY)] * 2,
        out_specs=pl.BlockSpec(memory_space=pltpu.VMEM),
        scratch_shapes=[
            pltpu.VMEM((slabs + 2, rows, width), b16),
            pltpu.VMEM((slabs, tall, width), f32),
            pltpu.VMEM((slabs + 2, local, width), b16),
            pltpu.VMEM((inner, terms * local, cells_dev), b16),
            pltpu.VMEM((rows, cells_dev), b16),
            pltpu.VMEM((terms * local, rows), f32),
        ]
        + [pltpu.VMEM((outer, n, rows), f32) for n in deep]
        + [pltpu.VMEM((outer - 1, n, rows), f32) for n in deep]
        + [
            pltpu.VMEM((tall, width), f32),
            pltpu.VMEM((outer - 1, tall, width), f32),
            pltpu.VMEM((tall, width), f32),
            pltpu.VMEM((inner - 1, tall, width), f32),
            dma((slabs_dev + 1,)),
            dma((inner - 1,)),
            dma((inner - 1,)),
            dma((inner - 1,)),
            dma((inner - 1,)),
            dma((2,)),
            dma((2,)),
            dma((terms * (outer - 1),)),
            dma((terms * (outer - 1),)),
            dma((outer - 1,)),
            dma((outer - 1,)),
            dma((inner - 1,)),
            dma((inner - 1,)),
        ],
        compiler_params=pltpu.CompilerParams(
            collective_id=0, has_side_effects=True, vmem_limit_bytes=48 << 20
        ),
    )(basis, kap)


def solution(mesh):
    return jax.shard_map(
        per_device,
        mesh=mesh,
        in_specs=(P("groups", "mode"), P(("groups", "mode")), P("groups", None), P("groups")),
        out_specs=P(None, ("groups", "mode"), None),
        check_vma=False,
    )
```

```python
import functools

import jax
import jax.numpy as jnp
from jax import lax
from jax.experimental import pallas as pl
from jax.experimental.pallas import tpu as pltpu
from jax.sharding import PartitionSpec as P


def plane_size(devices, share):
    size = 1
    while (
        4 * size * size <= 2 * devices
        and devices % (2 * size) == 0
        and 2 * size * share <= 24 << 20
    ):
        size *= 2
    return size


def slab_weights(slab_region, coef_index, coef_table):
    regions = coef_index.shape[0]
    entries = coef_table.shape[0]
    table_hit = (
        coef_index[:, :, None] == jnp.arange(entries, dtype=jnp.int32)[None, None, :]
    ).astype(jnp.float32)
    kappa = jnp.sum(table_hit * coef_table[None, None, :], axis=2)
    region_hit = (slab_region[:, None] == jnp.arange(regions, dtype=jnp.int32)[None, :]).astype(
        jnp.float32
    )
    return jnp.sum(region_hit[:, :, None] * kappa[None, :, :], axis=1)


def one_action(term, here, before, after, across, opposite, kappa):
    value = here.astype(jnp.float32)
    if term == 0:
        stencil = 2.0 * value - before.astype(jnp.float32) - after.astype(jnp.float32)
    elif term == 1:
        stencil = jnp.dot(here, across, preferred_element_type=jnp.float32)
    elif term == 2:
        stencil = value - before.astype(jnp.float32)
    elif term == 3:
        stencil = value - after.astype(jnp.float32)
    elif term == 4:
        stencil = jnp.dot(here, opposite, preferred_element_type=jnp.float32)
    else:
        stencil = value
    return (kappa * stencil).astype(jnp.bfloat16)


def gram_kernel(terms, inner, outer, own, slabs_dev, total_cells, *refs):
    basis, kap, out = refs[:3]
    field, weights, mine, lhs, act, acc = refs[3:9]
    stages = refs[9 : 9 + terms]
    arrived = refs[9 + terms : 9 + 2 * terms]
    lvl, lvl_col, lvl_mid, lvl_row = refs[9 + 2 * terms : 13 + 2 * terms]
    load_sem, gs, gr, ks, kr, hs, hr, zs, zr, cs, cr, rs, rr = refs[13 + 2 * terms :]
    rows, width = field.shape[1], field.shape[2]
    slabs = inner * slabs_dev
    local = outer * own
    me = lax.axis_index("mode")
    plane = me // inner
    column = me % inner

    def row_peer(d):
        return plane * inner + lax.rem(column + d, inner)

    def col_peer(d):
        return lax.rem(plane + d, outer) * inner + column

    def remote(src, dst, send, recv, peer):
        return pltpu.make_async_remote_copy(
            src_ref=src,
            dst_ref=dst,
            send_sem=send,
            recv_sem=recv,
            device_id={"mode": peer},
            device_id_type=pl.DeviceIdType.MESH,
        )

    loads = []
    for s in range(slabs_dev):
        loads.append(
            pltpu.make_async_copy(
                basis.at[:, pl.ds(s * width, width)],
                field.at[1 + column * slabs_dev + s],
                load_sem.at[s],
            )
        )
    loads.append(
        pltpu.make_async_copy(
            kap, weights.at[pl.ds(column * slabs_dev, slabs_dev)], load_sem.at[slabs_dev]
        )
    )
    for copy in loads:
        copy.start()

    barrier = pltpu.get_barrier_semaphore()
    for d in range(1, inner):
        pl.semaphore_signal(
            barrier, inc=1, device_id={"mode": row_peer(d)}, device_id_type=pl.DeviceIdType.MESH
        )
    for d in range(1, outer):
        pl.semaphore_signal(
            barrier, inc=1, device_id={"mode": col_peer(d)}, device_id_type=pl.DeviceIdType.MESH
        )
    pl.semaphore_wait(barrier, inner + outer - 2)
    for copy in loads:
        copy.wait()

    chips = inner // 2
    chip = column // 2
    core = column % 2
    sibling = plane * inner + chip * 2 + 1 - core
    spot = pl.ds(column * slabs_dev, slabs_dev)
    small = [
        remote(weights.at[spot], weights.at[spot], ks.at[d - 1], kr.at[d - 1], row_peer(d))
        for d in range(1, inner)
    ]

    def push(origin, slot, peer):
        span = pl.ds(1 + origin * slabs_dev, slabs_dev)
        return remote(field.at[span], field.at[span], gs.at[slot], gr.at[slot], peer)

    far = [
        push(column, d, plane * inner + lax.rem(chip + d, chips) * 2 + core)
        for d in range(1, chips)
    ]
    gathers = [push(column, 0, sibling)]
    for copy in small + far + gathers:
        copy.start()

    wi = lax.broadcasted_iota(jnp.int32, (width, width), 0)
    wj = lax.broadcasted_iota(jnp.int32, (width, width), 1)
    near = jnp.where((wi == wj + 1) | (wj == wi + 1), 1.0, 0.0)
    same = jnp.where(wi == wj, 1.0, 0.0)
    flip = jnp.where(wi + wj == width - 1, 1.0, 0.0)
    across = (2.0 * same - near).astype(jnp.bfloat16)
    opposite = (same - flip).astype(jnp.bfloat16)
    ri = lax.broadcasted_iota(jnp.int32, (local, rows), 0)
    rj = lax.broadcasted_iota(jnp.int32, (local, rows), 1)
    source = ri + column * own
    for a in range(1, outer):
        source = source + jnp.where(ri >= a * own, inner * own - own, 0)
    select = jnp.where(rj == source, 1.0, 0.0).astype(jnp.bfloat16)
    lvl[...] = jnp.zeros_like(lvl)

    def pick(first, count):
        for s in range(count):
            mine[first + s] = jnp.dot(
                select, field[first + s], preferred_element_type=jnp.float32
            ).astype(jnp.bfloat16)

    def own_actions(b, chosen):
        for term in chosen:
            squares = None
            for s in range(slabs_dev):
                at = b * slabs_dev + s
                value = one_action(
                    term,
                    mine[at + 1],
                    None if term in alone else mine[at],
                    None if term in alone else mine[at + 2],
                    across,
                    opposite,
                    weights[at, term : term + 1, :],
                )
                lhs[b, term * local : (term + 1) * local, s * width : (s + 1) * width] = value
                wide = value.astype(jnp.float32)
                squares = wide * wide if squares is None else squares + wide * wide
            lvl[term : term + 1, :] += jnp.sum(squares, axis=0, keepdims=True)

    alone = (1, 4, 5)
    coupled = tuple(term for term in range(terms) if term not in alone)

    def settle(origin):
        pick(1 + origin * slabs_dev, slabs_dev)
        own_actions(origin, alone)

    for copy in small:
        copy.wait()
    settle(column)
    gathers[0].wait()
    settle(chip * 2 + 1 - core)
    for d, copy in enumerate(far, 1):
        copy.wait_recv()
        origin = lax.rem(chip + chips - d, chips) * 2 + core
        relay = push(origin, chips - 1 + d, sibling)
        relay.start()
        gathers.append(relay)
        settle(origin)
    for copy in far:
        copy.wait_send()
    for copy in gathers[1:]:
        copy.wait()
    halos = [
        remote(field.at[slabs], field.at[0], hs.at[0], hr.at[0], col_peer(1)),
        remote(field.at[1], field.at[slabs + 1], hs.at[1], hr.at[1], col_peer(outer - 1)),
    ]
    for copy in halos:
        copy.start()
    for d in range(1, chips):
        settle(lax.rem(chip + chips - d, chips) * 2 + 1 - core)

    @pl.loop(1, inner - 1)
    def _(b):
        own_actions(b, coupled)

    for copy in halos:
        copy.wait()
    pick(0, 1)
    pick(slabs + 1, 1)
    own_actions(0, coupled)
    own_actions(inner - 1, coupled)

    cols = [
        remote(lvl, lvl_col.at[d - 1], cs.at[d - 1], cr.at[d - 1], col_peer(d))
        for d in range(1, outer)
    ]
    for copy in cols:
        copy.start()

    sends = []
    rowsends = []
    for turn, second in enumerate(reversed(range(terms))):
        deep = (second + 1) * local
        acc[0:deep, :] = jnp.zeros((deep, rows), jnp.float32)

        @pl.loop(0, inner)
        def _(b, second=second, deep=deep):
            for s in range(slabs_dev):
                at = b * slabs_dev + s
                act[:, s * width : (s + 1) * width] = one_action(
                    second,
                    field[at + 1],
                    field[at],
                    field[at + 2],
                    across,
                    opposite,
                    weights[at, second : second + 1, :],
                )
            acc[0:deep, :] += lax.dot_general(
                lhs[b, 0:deep, :],
                act[...],
                (((1,), (1,)), ((), ())),
                preferred_element_type=jnp.float32,
            )

        for a in range(outer):
            for first in range(second + 1):
                stages[second][a, first * own : (first + 1) * own, :] = acc[
                    first * local + a * own : first * local + (a + 1) * own, :
                ]
        for d in range(1, outer):
            n = second * (outer - 1) + d - 1
            copy = remote(
                stages[second].at[lax.rem(plane + d, outer)],
                arrived[second].at[d - 1],
                zs.at[n],
                zr.at[n],
                col_peer(d),
            )
            copy.start()
            sends.append((second, copy))
        if turn == 0:
            for copy in cols:
                copy.wait()
            mid = lvl[...]
            for d in range(1, outer):
                mid = mid + lvl_col[d - 1]
            lvl_mid[...] = mid
            rowsends = [
                remote(lvl_mid, lvl_row.at[d - 1], rs.at[d - 1], rr.at[d - 1], row_peer(d))
                for d in range(1, inner)
            ]
            for copy in rowsends:
                copy.start()

    for copy in rowsends:
        copy.wait()
    total = lvl_mid[...]
    for d in range(1, inner):
        total = total + lvl_row[d - 1]
    level = jnp.sum(total, axis=1, keepdims=True) / (rows * total_cells) + 1e-06
    for second in reversed(range(terms)):
        for q, copy in sends:
            if q == second:
                copy.wait()
        for first in range(second + 1):
            part = pl.ds(first * own, own)
            value = stages[second][plane, part, :]
            for d in range(1, outer):
                value = value + arrived[second][d - 1, part, :]
            factor = 1.0 / (
                total_cells * jnp.sqrt(level[first : first + 1] * level[second : second + 1])
            )
            pair = first * terms - first * (first - 1) // 2 + second - first
            out[pair] = value * factor


def per_device(basis, slab_region, coef_index, coef_table):
    terms = coef_index.shape[1]
    rows, cells_dev = basis.shape
    slabs_dev = slab_region.shape[0]
    width = cells_dev // slabs_dev
    devices = lax.axis_size("mode")
    inner = plane_size(devices, 2 * terms * rows * cells_dev)
    outer = devices // inner
    own = rows // devices
    slabs = slabs_dev * inner
    local = outer * own
    slab_kappa = slab_weights(slab_region, coef_index, coef_table)
    kap = jnp.broadcast_to(
        jnp.pad(slab_kappa, ((0, 0), (0, -terms % 8)))[:, :, None],
        (slabs_dev, terms + -terms % 8, width),
    )
    tall = terms + -terms % 8
    f32, b16 = jnp.float32, jnp.bfloat16
    deep = [(q + 1) * own for q in range(terms)]
    dma = pltpu.SemaphoreType.DMA
    return pl.pallas_call(
        functools.partial(
            gram_kernel, terms, inner, outer, own, slabs_dev, cells_dev * devices
        ),
        out_shape=jax.ShapeDtypeStruct((terms * (terms + 1) // 2, own, rows), f32),
        in_specs=[pl.BlockSpec(memory_space=pl.ANY)] * 2,
        out_specs=pl.BlockSpec(memory_space=pltpu.VMEM),
        scratch_shapes=[
            pltpu.VMEM((slabs + 2, rows, width), b16),
            pltpu.VMEM((slabs, tall, width), f32),
            pltpu.VMEM((slabs + 2, local, width), b16),
            pltpu.VMEM((inner, terms * local, cells_dev), b16),
            pltpu.VMEM((rows, cells_dev), b16),
            pltpu.VMEM((terms * local, rows), f32),
        ]
        + [pltpu.VMEM((outer, n, rows), f32) for n in deep]
        + [pltpu.VMEM((outer - 1, n, rows), f32) for n in deep]
        + [
            pltpu.VMEM((tall, width), f32),
            pltpu.VMEM((outer - 1, tall, width), f32),
            pltpu.VMEM((tall, width), f32),
            pltpu.VMEM((inner - 1, tall, width), f32),
            dma((slabs_dev + 1,)),
            dma((inner - 1,)),
            dma((inner - 1,)),
            dma((inner - 1,)),
            dma((inner - 1,)),
            dma((2,)),
            dma((2,)),
            dma((terms * (outer - 1),)),
            dma((terms * (outer - 1),)),
            dma((outer - 1,)),
            dma((outer - 1,)),
            dma((inner - 1,)),
            dma((inner - 1,)),
        ],
        compiler_params=pltpu.CompilerParams(
            collective_id=0, has_side_effects=True, vmem_limit_bytes=48 << 20
        ),
    )(basis, kap)


def solution(mesh):
    return jax.shard_map(
        per_device,
        mesh=mesh,
        in_specs=(P("groups", "mode"), P(("groups", "mode")), P("groups", None), P("groups")),
        out_specs=P(None, ("groups", "mode"), None),
        check_vma=False,
    )
```

```python
import functools

import jax
import jax.numpy as jnp
from jax import lax
from jax.experimental import pallas as pl
from jax.experimental.pallas import tpu as pltpu
from jax.sharding import PartitionSpec as P


def plane_size(devices, share):
    size = 1
    while (
        4 * size * size <= 2 * devices
        and devices % (2 * size) == 0
        and 2 * size * share <= 24 << 20
    ):
        size *= 2
    return size


def slab_weights(slab_region, coef_index, coef_table):
    regions = coef_index.shape[0]
    entries = coef_table.shape[0]
    table_hit = (
        coef_index[:, :, None] == jnp.arange(entries, dtype=jnp.int32)[None, None, :]
    ).astype(jnp.float32)
    kappa = jnp.sum(table_hit * coef_table[None, None, :], axis=2)
    region_hit = (slab_region[:, None] == jnp.arange(regions, dtype=jnp.int32)[None, :]).astype(
        jnp.float32
    )
    return jnp.sum(region_hit[:, :, None] * kappa[None, :, :], axis=1)


def one_action(term, here, before, after, across, opposite, kappa):
    value = here.astype(jnp.float32)
    if term == 0:
        stencil = 2.0 * value - before.astype(jnp.float32) - after.astype(jnp.float32)
    elif term == 1:
        stencil = jnp.dot(here, across, preferred_element_type=jnp.float32)
    elif term == 2:
        stencil = value - before.astype(jnp.float32)
    elif term == 3:
        stencil = value - after.astype(jnp.float32)
    elif term == 4:
        stencil = jnp.dot(here, opposite, preferred_element_type=jnp.float32)
    else:
        stencil = value
    return (kappa * stencil).astype(jnp.bfloat16)


def gram_kernel(terms, inner, outer, own, slabs_dev, total_cells, *refs):
    basis, kap, out = refs[:3]
    field, weights, mine, lhs, act, acc = refs[3:9]
    stages = refs[9 : 9 + terms]
    arrived = refs[9 + terms : 9 + 2 * terms]
    codes = refs[9 + 2 * terms : 9 + 3 * terms]
    scales = refs[9 + 3 * terms : 9 + 4 * terms]
    got_scales = refs[9 + 4 * terms : 9 + 5 * terms]
    lvl, lvl_col, lvl_mid, lvl_row, whole, ss, sr = refs[9 + 5 * terms : 16 + 5 * terms]
    load_sem, gs, gr, ks, kr, hs, hr, zs, zr, cs, cr, rs, rr = refs[16 + 5 * terms :]
    rows, width = field.shape[1], field.shape[2]
    slabs = inner * slabs_dev
    local = outer * own
    me = lax.axis_index("mode")
    plane = me // inner
    column = me % inner

    def row_peer(d):
        return plane * inner + lax.rem(column + d, inner)

    def col_peer(d):
        return lax.rem(plane + d, outer) * inner + column

    def remote(src, dst, send, recv, peer):
        return pltpu.make_async_remote_copy(
            src_ref=src,
            dst_ref=dst,
            send_sem=send,
            recv_sem=recv,
            device_id={"mode": peer},
            device_id_type=pl.DeviceIdType.MESH,
        )

    loads = []
    for s in range(slabs_dev):
        loads.append(
            pltpu.make_async_copy(
                basis.at[:, pl.ds(s * width, width)],
                field.at[1 + column * slabs_dev + s],
                load_sem.at[s],
            )
        )
    loads.append(
        pltpu.make_async_copy(
            kap, weights.at[pl.ds(column * slabs_dev, slabs_dev)], load_sem.at[slabs_dev]
        )
    )
    for copy in loads:
        copy.start()

    barrier = pltpu.get_barrier_semaphore()
    for d in range(1, inner):
        pl.semaphore_signal(
            barrier, inc=1, device_id={"mode": row_peer(d)}, device_id_type=pl.DeviceIdType.MESH
        )
    for d in range(1, outer):
        pl.semaphore_signal(
            barrier, inc=1, device_id={"mode": col_peer(d)}, device_id_type=pl.DeviceIdType.MESH
        )
    pl.semaphore_wait(barrier, inner + outer - 2)
    for copy in loads:
        copy.wait()

    chips = inner // 2
    chip = column // 2
    core = column % 2
    sibling = plane * inner + chip * 2 + 1 - core
    spot = pl.ds(column * slabs_dev, slabs_dev)
    small = [
        remote(weights.at[spot], weights.at[spot], ks.at[d - 1], kr.at[d - 1], row_peer(d))
        for d in range(1, inner)
    ]

    def push(origin, slot, peer):
        span = pl.ds(1 + origin * slabs_dev, slabs_dev)
        return remote(field.at[span], field.at[span], gs.at[slot], gr.at[slot], peer)

    far = [
        push(column, d, plane * inner + lax.rem(chip + d, chips) * 2 + core)
        for d in range(1, chips)
    ]
    gathers = [push(column, 0, sibling)]
    for copy in small + far + gathers:
        copy.start()

    wi = lax.broadcasted_iota(jnp.int32, (width, width), 0)
    wj = lax.broadcasted_iota(jnp.int32, (width, width), 1)
    near = jnp.where((wi == wj + 1) | (wj == wi + 1), 1.0, 0.0)
    same = jnp.where(wi == wj, 1.0, 0.0)
    flip = jnp.where(wi + wj == width - 1, 1.0, 0.0)
    across = (2.0 * same - near).astype(jnp.bfloat16)
    opposite = (same - flip).astype(jnp.bfloat16)
    ri = lax.broadcasted_iota(jnp.int32, (local, rows), 0)
    rj = lax.broadcasted_iota(jnp.int32, (local, rows), 1)
    source = ri + column * own
    for a in range(1, outer):
        source = source + jnp.where(ri >= a * own, inner * own - own, 0)
    select = jnp.where(rj == source, 1.0, 0.0).astype(jnp.bfloat16)
    lvl[...] = jnp.zeros_like(lvl)

    def pick(first, count):
        for s in range(count):
            mine[first + s] = jnp.dot(
                select, field[first + s], preferred_element_type=jnp.float32
            ).astype(jnp.bfloat16)

    def own_actions(b, chosen):
        for term in chosen:
            squares = None
            for s in range(slabs_dev):
                at = b * slabs_dev + s
                value = one_action(
                    term,
                    mine[at + 1],
                    None if term in alone else mine[at],
                    None if term in alone else mine[at + 2],
                    across,
                    opposite,
                    weights[at, term : term + 1, :],
                )
                lhs[b, term * local : (term + 1) * local, s * width : (s + 1) * width] = value
                wide = value.astype(jnp.float32)
                squares = wide * wide if squares is None else squares + wide * wide
            lvl[term : term + 1, :] += jnp.sum(squares, axis=0, keepdims=True)

    alone = (1, 4, 5)
    coupled = tuple(term for term in range(terms) if term not in alone)

    def settle(origin):
        pick(1 + origin * slabs_dev, slabs_dev)
        own_actions(origin, alone)

    for copy in small:
        copy.wait()
    settle(column)
    gathers[0].wait()
    settle(chip * 2 + 1 - core)
    for d, copy in enumerate(far, 1):
        copy.wait_recv()
        origin = lax.rem(chip + chips - d, chips) * 2 + core
        relay = push(origin, chips - 1 + d, sibling)
        relay.start()
        gathers.append(relay)
        settle(origin)
    for copy in far:
        copy.wait_send()
    for copy in gathers[1:]:
        copy.wait()
    halos = [
        remote(field.at[slabs], field.at[0], hs.at[0], hr.at[0], col_peer(1)),
        remote(field.at[1], field.at[slabs + 1], hs.at[1], hr.at[1], col_peer(outer - 1)),
    ]
    for copy in halos:
        copy.start()
    for d in range(1, chips):
        settle(lax.rem(chip + chips - d, chips) * 2 + 1 - core)

    @pl.loop(1, inner - 1)
    def _(b):
        own_actions(b, coupled)

    for copy in halos:
        copy.wait()
    pick(0, 1)
    pick(slabs + 1, 1)
    own_actions(0, coupled)
    own_actions(inner - 1, coupled)

    cols = [
        remote(lvl, lvl_col.at[d - 1], cs.at[d - 1], cr.at[d - 1], col_peer(d))
        for d in range(1, outer)
    ]
    for copy in cols:
        copy.start()

    sends = []
    rowsends = []
    for turn, second in enumerate(reversed(range(terms))):
        deep = (second + 1) * local
        acc[0:deep, :] = jnp.zeros((deep, rows), jnp.float32)

        @pl.loop(0, inner)
        def _(b, second=second, deep=deep):
            for s in range(slabs_dev):
                at = b * slabs_dev + s
                act[:, s * width : (s + 1) * width] = one_action(
                    second,
                    field[at + 1],
                    field[at],
                    field[at + 2],
                    across,
                    opposite,
                    weights[at, second : second + 1, :],
                )
            acc[0:deep, :] += lax.dot_general(
                lhs[b, 0:deep, :],
                act[...],
                (((1,), (1,)), ((), ())),
                preferred_element_type=jnp.float32,
            )

        for a in range(outer):
            for first in range(second + 1):
                value = acc[first * local + a * own : first * local + (a + 1) * own, :]
                stages[second][a, first * own : (first + 1) * own, :] = value
                peak = jnp.max(jnp.abs(value), axis=0, keepdims=True)
                scale = peak * (1.0 / 32000.0)
                scale = jnp.where(scale > 0.0, scale, 1.0)
                scales[second][a, first : first + 1, :] = scale
                whole[first * own : (first + 1) * own, :] = jnp.round(
                    jnp.clip(value / scale, -32767.0, 32767.0)
                )
            codes[second][a] = (
                whole[0 : (second + 1) * own, :].astype(jnp.int32).astype(jnp.int16)
            )
        for d in range(1, outer):
            n = second * (outer - 1) + d - 1
            scale_copy = remote(
                scales[second].at[lax.rem(plane + d, outer)],
                got_scales[second].at[d - 1],
                ss.at[n],
                sr.at[n],
                col_peer(d),
            )
            scale_copy.start()
            sends.append((second, scale_copy))
            copy = remote(
                codes[second].at[lax.rem(plane + d, outer)],
                arrived[second].at[d - 1],
                zs.at[n],
                zr.at[n],
                col_peer(d),
            )
            copy.start()
            sends.append((second, copy))
        if turn == 0:
            for copy in cols:
                copy.wait()
            mid = lvl[...]
            for d in range(1, outer):
                mid = mid + lvl_col[d - 1]
            lvl_mid[...] = mid
            rowsends = [
                remote(lvl_mid, lvl_row.at[d - 1], rs.at[d - 1], rr.at[d - 1], row_peer(d))
                for d in range(1, inner)
            ]
            for copy in rowsends:
                copy.start()

    for copy in rowsends:
        copy.wait()
    total = lvl_mid[...]
    for d in range(1, inner):
        total = total + lvl_row[d - 1]
    level = jnp.sum(total, axis=1, keepdims=True) / (rows * total_cells) + 1e-06
    for second in reversed(range(terms)):
        for q, copy in sends:
            if q == second:
                copy.wait()
        opened = [
            arrived[second][d - 1].astype(jnp.int32).astype(jnp.float32)
            for d in range(1, outer)
        ]
        for first in range(second + 1):
            part = pl.ds(first * own, own)
            value = stages[second][plane, part, :]
            for d in range(1, outer):
                value = value + (
                    opened[d - 1][first * own : (first + 1) * own, :]
                    * got_scales[second][d - 1, first : first + 1, :]
                )
            factor = 1.0 / (
                total_cells * jnp.sqrt(level[first : first + 1] * level[second : second + 1])
            )
            pair = first * terms - first * (first - 1) // 2 + second - first
            out[pair] = value * factor


def per_device(basis, slab_region, coef_index, coef_table):
    terms = coef_index.shape[1]
    rows, cells_dev = basis.shape
    slabs_dev = slab_region.shape[0]
    width = cells_dev // slabs_dev
    devices = lax.axis_size("mode")
    inner = plane_size(devices, 2 * terms * rows * cells_dev)
    outer = devices // inner
    own = rows // devices
    slabs = slabs_dev * inner
    local = outer * own
    slab_kappa = slab_weights(slab_region, coef_index, coef_table)
    kap = jnp.broadcast_to(
        jnp.pad(slab_kappa, ((0, 0), (0, -terms % 8)))[:, :, None],
        (slabs_dev, terms + -terms % 8, width),
    )
    tall = terms + -terms % 8
    f32, b16 = jnp.float32, jnp.bfloat16
    deep = [(q + 1) * own for q in range(terms)]
    dma = pltpu.SemaphoreType.DMA
    return pl.pallas_call(
        functools.partial(
            gram_kernel, terms, inner, outer, own, slabs_dev, cells_dev * devices
        ),
        out_shape=jax.ShapeDtypeStruct((terms * (terms + 1) // 2, own, rows), f32),
        in_specs=[pl.BlockSpec(memory_space=pl.ANY)] * 2,
        out_specs=pl.BlockSpec(memory_space=pltpu.VMEM),
        scratch_shapes=[
            pltpu.VMEM((slabs + 2, rows, width), b16),
            pltpu.VMEM((slabs, tall, width), f32),
            pltpu.VMEM((slabs + 2, local, width), b16),
            pltpu.VMEM((inner, terms * local, cells_dev), b16),
            pltpu.VMEM((rows, cells_dev), b16),
            pltpu.VMEM((terms * local, rows), f32),
        ]
        + [pltpu.VMEM((outer, n, rows), f32) for n in deep]
        + [pltpu.VMEM((outer - 1, n, rows), jnp.int16) for n in deep]
        + [pltpu.VMEM((outer, n, rows), jnp.int16) for n in deep]
        + [pltpu.VMEM((outer, n + 1, rows), f32) for n in range(terms)]
        + [pltpu.VMEM((outer - 1, n + 1, rows), f32) for n in range(terms)]
        + [
            pltpu.VMEM((tall, width), f32),
            pltpu.VMEM((outer - 1, tall, width), f32),
            pltpu.VMEM((tall, width), f32),
            pltpu.VMEM((inner - 1, tall, width), f32),
            pltpu.VMEM((deep[-1], rows), f32),
            dma((terms * (outer - 1),)),
            dma((terms * (outer - 1),)),
            dma((slabs_dev + 1,)),
            dma((inner - 1,)),
            dma((inner - 1,)),
            dma((inner - 1,)),
            dma((inner - 1,)),
            dma((2,)),
            dma((2,)),
            dma((terms * (outer - 1),)),
            dma((terms * (outer - 1),)),
            dma((outer - 1,)),
            dma((outer - 1,)),
            dma((inner - 1,)),
            dma((inner - 1,)),
        ],
        compiler_params=pltpu.CompilerParams(
            collective_id=0, has_side_effects=True, vmem_limit_bytes=48 << 20
        ),
    )(basis, kap)


def solution(mesh):
    return jax.shard_map(
        per_device,
        mesh=mesh,
        in_specs=(P("groups", "mode"), P(("groups", "mode")), P("groups", None), P("groups")),
        out_specs=P(None, ("groups", "mode"), None),
        check_vma=False,
    )
```

```python
import functools

import jax
import jax.numpy as jnp
from jax import lax
from jax.experimental import pallas as pl
from jax.experimental.pallas import tpu as pltpu
from jax.sharding import PartitionSpec as P


def plane_size(devices, share):
    size = 1
    while (
        4 * size * size <= 2 * devices
        and devices % (2 * size) == 0
        and 2 * size * share <= 24 << 20
    ):
        size *= 2
    return size


def slab_weights(slab_region, coef_index, coef_table):
    regions = coef_index.shape[0]
    entries = coef_table.shape[0]
    table_hit = (
        coef_index[:, :, None] == jnp.arange(entries, dtype=jnp.int32)[None, None, :]
    ).astype(jnp.float32)
    kappa = jnp.sum(table_hit * coef_table[None, None, :], axis=2)
    region_hit = (slab_region[:, None] == jnp.arange(regions, dtype=jnp.int32)[None, :]).astype(
        jnp.float32
    )
    return jnp.sum(region_hit[:, :, None] * kappa[None, :, :], axis=1)


def one_action(term, here, before, after, across, opposite, kappa):
    value = here.astype(jnp.float32)
    if term == 0:
        stencil = 2.0 * value - before.astype(jnp.float32) - after.astype(jnp.float32)
    elif term == 1:
        stencil = jnp.dot(here, across, preferred_element_type=jnp.float32)
    elif term == 2:
        stencil = value - before.astype(jnp.float32)
    elif term == 3:
        stencil = value - after.astype(jnp.float32)
    elif term == 4:
        stencil = jnp.dot(here, opposite, preferred_element_type=jnp.float32)
    else:
        stencil = value
    return (kappa * stencil).astype(jnp.bfloat16)


def gram_kernel(terms, inner, outer, own, slabs_dev, total_cells, *refs):
    basis, kap, out = refs[:3]
    field, weights, mine, lhs, act, acc = refs[3:9]
    stages = refs[9 : 9 + terms]
    arrived = refs[9 + terms : 9 + 2 * terms]
    codes = refs[9 + 2 * terms : 9 + 3 * terms]
    scales = refs[9 + 3 * terms : 9 + 4 * terms]
    got_scales = refs[9 + 4 * terms : 9 + 5 * terms]
    lvl, lvl_col, lvl_mid, lvl_row, whole, ss, sr = refs[9 + 5 * terms : 16 + 5 * terms]
    load_sem, gs, gr, ks, kr, hs, hr, zs, zr, cs, cr, rs, rr = refs[16 + 5 * terms :]
    rows, width = field.shape[1], field.shape[2]
    slabs = inner * slabs_dev
    local = outer * own
    me = lax.axis_index("mode")
    plane = me // inner
    column = me % inner

    def row_peer(d):
        return plane * inner + lax.rem(column + d, inner)

    def col_peer(d):
        return lax.rem(plane + d, outer) * inner + column

    def remote(src, dst, send, recv, peer):
        return pltpu.make_async_remote_copy(
            src_ref=src,
            dst_ref=dst,
            send_sem=send,
            recv_sem=recv,
            device_id={"mode": peer},
            device_id_type=pl.DeviceIdType.MESH,
        )

    loads = []
    for s in range(slabs_dev):
        loads.append(
            pltpu.make_async_copy(
                basis.at[:, pl.ds(s * width, width)],
                field.at[1 + column * slabs_dev + s],
                load_sem.at[s],
            )
        )
    loads.append(
        pltpu.make_async_copy(
            kap, weights.at[pl.ds(column * slabs_dev, slabs_dev)], load_sem.at[slabs_dev]
        )
    )
    for copy in loads:
        copy.start()

    barrier = pltpu.get_barrier_semaphore()
    for d in range(1, inner):
        pl.semaphore_signal(
            barrier, inc=1, device_id={"mode": row_peer(d)}, device_id_type=pl.DeviceIdType.MESH
        )
    for d in range(1, outer):
        pl.semaphore_signal(
            barrier, inc=1, device_id={"mode": col_peer(d)}, device_id_type=pl.DeviceIdType.MESH
        )
    pl.semaphore_wait(barrier, inner + outer - 2)
    for copy in loads:
        copy.wait()

    chips = inner // 2
    chip = column // 2
    core = column % 2
    sibling = plane * inner + chip * 2 + 1 - core
    spot = pl.ds(column * slabs_dev, slabs_dev)
    small = [
        remote(weights.at[spot], weights.at[spot], ks.at[d - 1], kr.at[d - 1], row_peer(d))
        for d in range(1, inner)
    ]

    def push(origin, slot, peer):
        span = pl.ds(1 + origin * slabs_dev, slabs_dev)
        return remote(field.at[span], field.at[span], gs.at[slot], gr.at[slot], peer)

    far = [
        push(column, d, plane * inner + lax.rem(chip + d, chips) * 2 + core)
        for d in range(1, chips)
    ]
    gathers = [push(column, 0, sibling)]
    for copy in small + far + gathers:
        copy.start()

    wi = lax.broadcasted_iota(jnp.int32, (width, width), 0)
    wj = lax.broadcasted_iota(jnp.int32, (width, width), 1)
    near = jnp.where((wi == wj + 1) | (wj == wi + 1), 1.0, 0.0)
    same = jnp.where(wi == wj, 1.0, 0.0)
    flip = jnp.where(wi + wj == width - 1, 1.0, 0.0)
    across = (2.0 * same - near).astype(jnp.bfloat16)
    opposite = (same - flip).astype(jnp.bfloat16)
    ri = lax.broadcasted_iota(jnp.int32, (local, rows), 0)
    rj = lax.broadcasted_iota(jnp.int32, (local, rows), 1)
    source = ri + column * own
    for a in range(1, outer):
        source = source + jnp.where(ri >= a * own, inner * own - own, 0)
    select = jnp.where(rj == source, 1.0, 0.0).astype(jnp.bfloat16)
    lvl[...] = jnp.zeros_like(lvl)

    def pick(first, count):
        for s in range(count):
            mine[first + s] = jnp.dot(
                select, field[first + s], preferred_element_type=jnp.float32
            ).astype(jnp.bfloat16)

    def own_actions(b, chosen):
        for term in chosen:
            squares = None
            for s in range(slabs_dev):
                at = b * slabs_dev + s
                value = one_action(
                    term,
                    mine[at + 1],
                    None if term in alone else mine[at],
                    None if term in alone else mine[at + 2],
                    across,
                    opposite,
                    weights[at, term : term + 1, :],
                )
                lhs[b, term * local : (term + 1) * local, s * width : (s + 1) * width] = value
                wide = value.astype(jnp.float32)
                squares = wide * wide if squares is None else squares + wide * wide
            lvl[term : term + 1, :] += jnp.sum(squares, axis=0, keepdims=True)

    alone = (1, 4, 5)
    coupled = tuple(term for term in range(terms) if term not in alone)

    def settle(origin):
        pick(1 + origin * slabs_dev, slabs_dev)
        own_actions(origin, alone)

    for copy in small:
        copy.wait()
    settle(column)
    gathers[0].wait()
    settle(chip * 2 + 1 - core)
    for d, copy in enumerate(far, 1):
        copy.wait_recv()
        origin = lax.rem(chip + chips - d, chips) * 2 + core
        relay = push(origin, chips - 1 + d, sibling)
        relay.start()
        gathers.append(relay)
        settle(origin)
    for copy in far:
        copy.wait_send()
    for copy in gathers[1:]:
        copy.wait()
    halos = [
        remote(field.at[slabs], field.at[0], hs.at[0], hr.at[0], col_peer(1)),
        remote(field.at[1], field.at[slabs + 1], hs.at[1], hr.at[1], col_peer(outer - 1)),
    ]
    for copy in halos:
        copy.start()
    for d in range(1, chips):
        settle(lax.rem(chip + chips - d, chips) * 2 + 1 - core)

    @pl.loop(1, inner - 1)
    def _(b):
        own_actions(b, coupled)

    for copy in halos:
        copy.wait()
    pick(0, 1)
    pick(slabs + 1, 1)
    own_actions(0, coupled)
    own_actions(inner - 1, coupled)

    cols = [
        remote(lvl, lvl_col.at[d - 1], cs.at[d - 1], cr.at[d - 1], col_peer(d))
        for d in range(1, outer)
    ]
    for copy in cols:
        copy.start()

    sends = []
    rowsends = []
    for turn, second in enumerate(reversed(range(terms))):
        deep = (second + 1) * local
        acc[0:deep, :] = jnp.zeros((deep, rows), jnp.float32)

        @pl.loop(0, inner // 2)
        def _(half, second=second, deep=deep):
            for u in range(2):
                for s in range(slabs_dev):
                    at = (half * 2 + u) * slabs_dev + s
                    act[u, :, s * width : (s + 1) * width] = one_action(
                        second,
                        field[at + 1],
                        field[at],
                        field[at + 2],
                        across,
                        opposite,
                        weights[at, second : second + 1, :],
                    )
            sums = [
                lax.dot_general(
                    lhs[half * 2 + u, 0:deep, :],
                    act[u],
                    (((1,), (1,)), ((), ())),
                    preferred_element_type=jnp.float32,
                )
                for u in range(2)
            ]
            acc[0:deep, :] += sums[0] + sums[1]

        for a in range(outer):
            for first in range(second + 1):
                value = acc[first * local + a * own : first * local + (a + 1) * own, :]
                stages[second][a, first * own : (first + 1) * own, :] = value
                peak = jnp.max(jnp.abs(value), axis=0, keepdims=True)
                scale = peak * (1.0 / 32000.0)
                scale = jnp.where(scale > 0.0, scale, 1.0)
                scales[second][a, first : first + 1, :] = scale
                whole[first * own : (first + 1) * own, :] = jnp.round(
                    jnp.clip(value / scale, -32767.0, 32767.0)
                )
            codes[second][a] = (
                whole[0 : (second + 1) * own, :].astype(jnp.int32).astype(jnp.int16)
            )
        for d in range(1, outer):
            n = second * (outer - 1) + d - 1
            scale_copy = remote(
                scales[second].at[lax.rem(plane + d, outer)],
                got_scales[second].at[d - 1],
                ss.at[n],
                sr.at[n],
                col_peer(d),
            )
            scale_copy.start()
            sends.append((second, scale_copy))
            copy = remote(
                codes[second].at[lax.rem(plane + d, outer)],
                arrived[second].at[d - 1],
                zs.at[n],
                zr.at[n],
                col_peer(d),
            )
            copy.start()
            sends.append((second, copy))
        if turn == 0:
            for copy in cols:
                copy.wait()
            mid = lvl[...]
            for d in range(1, outer):
                mid = mid + lvl_col[d - 1]
            lvl_mid[...] = mid
            rowsends = [
                remote(lvl_mid, lvl_row.at[d - 1], rs.at[d - 1], rr.at[d - 1], row_peer(d))
                for d in range(1, inner)
            ]
            for copy in rowsends:
                copy.start()

    for copy in rowsends:
        copy.wait()
    total = lvl_mid[...]
    for d in range(1, inner):
        total = total + lvl_row[d - 1]
    level = jnp.sum(total, axis=1, keepdims=True) / (rows * total_cells) + 1e-06
    for second in reversed(range(terms)):
        for q, copy in sends:
            if q == second:
                copy.wait()
        opened = [
            arrived[second][d - 1].astype(jnp.int32).astype(jnp.float32)
            for d in range(1, outer)
        ]
        for first in range(second + 1):
            part = pl.ds(first * own, own)
            value = stages[second][plane, part, :]
            for d in range(1, outer):
                value = value + (
                    opened[d - 1][first * own : (first + 1) * own, :]
                    * got_scales[second][d - 1, first : first + 1, :]
                )
            factor = 1.0 / (
                total_cells * jnp.sqrt(level[first : first + 1] * level[second : second + 1])
            )
            pair = first * terms - first * (first - 1) // 2 + second - first
            out[pair] = value * factor


def per_device(basis, slab_region, coef_index, coef_table):
    terms = coef_index.shape[1]
    rows, cells_dev = basis.shape
    slabs_dev = slab_region.shape[0]
    width = cells_dev // slabs_dev
    devices = lax.axis_size("mode")
    inner = plane_size(devices, 2 * terms * rows * cells_dev)
    outer = devices // inner
    own = rows // devices
    slabs = slabs_dev * inner
    local = outer * own
    slab_kappa = slab_weights(slab_region, coef_index, coef_table)
    kap = jnp.broadcast_to(
        jnp.pad(slab_kappa, ((0, 0), (0, -terms % 8)))[:, :, None],
        (slabs_dev, terms + -terms % 8, width),
    )
    tall = terms + -terms % 8
    f32, b16 = jnp.float32, jnp.bfloat16
    deep = [(q + 1) * own for q in range(terms)]
    dma = pltpu.SemaphoreType.DMA
    return pl.pallas_call(
        functools.partial(
            gram_kernel, terms, inner, outer, own, slabs_dev, cells_dev * devices
        ),
        out_shape=jax.ShapeDtypeStruct((terms * (terms + 1) // 2, own, rows), f32),
        in_specs=[pl.BlockSpec(memory_space=pl.ANY)] * 2,
        out_specs=pl.BlockSpec(memory_space=pltpu.VMEM),
        scratch_shapes=[
            pltpu.VMEM((slabs + 2, rows, width), b16),
            pltpu.VMEM((slabs, tall, width), f32),
            pltpu.VMEM((slabs + 2, local, width), b16),
            pltpu.VMEM((inner, terms * local, cells_dev), b16),
            pltpu.VMEM((2, rows, cells_dev), b16),
            pltpu.VMEM((terms * local, rows), f32),
        ]
        + [pltpu.VMEM((outer, n, rows), f32) for n in deep]
        + [pltpu.VMEM((outer - 1, n, rows), jnp.int16) for n in deep]
        + [pltpu.VMEM((outer, n, rows), jnp.int16) for n in deep]
        + [pltpu.VMEM((outer, n + 1, rows), f32) for n in range(terms)]
        + [pltpu.VMEM((outer - 1, n + 1, rows), f32) for n in range(terms)]
        + [
            pltpu.VMEM((tall, width), f32),
            pltpu.VMEM((outer - 1, tall, width), f32),
            pltpu.VMEM((tall, width), f32),
            pltpu.VMEM((inner - 1, tall, width), f32),
            pltpu.VMEM((deep[-1], rows), f32),
            dma((terms * (outer - 1),)),
            dma((terms * (outer - 1),)),
            dma((slabs_dev + 1,)),
            dma((inner - 1,)),
            dma((inner - 1,)),
            dma((inner - 1,)),
            dma((inner - 1,)),
            dma((2,)),
            dma((2,)),
            dma((terms * (outer - 1),)),
            dma((terms * (outer - 1),)),
            dma((outer - 1,)),
            dma((outer - 1,)),
            dma((inner - 1,)),
            dma((inner - 1,)),
        ],
        compiler_params=pltpu.CompilerParams(
            collective_id=0, has_side_effects=True, vmem_limit_bytes=48 << 20
        ),
    )(basis, kap)


def solution(mesh):
    return jax.shard_map(
        per_device,
        mesh=mesh,
        in_specs=(P("groups", "mode"), P(("groups", "mode")), P("groups", None), P("groups")),
        out_specs=P(None, ("groups", "mode"), None),
        check_vma=False,
    )
```
